32 devices in a mesh: seq: 8 (over z, y), head: 4 (over x, core).
Axes of the slice: x: 2, y: 2, z: 4, core: 2. Of those that a mesh axis runs over, the one named last changes fastest.
Arguments:
- queries: bfloat16 [2048, 4096], P(('seq', 'head')), may hold values from -6 to 6
- keys_in: bfloat16 [2048, 4096], P(('seq', 'head')), may hold values from -6 to 6
- values_in: bfloat16 [2048, 4096], P(('seq', 'head')), may hold values from -8 to 8, as said below
- gain: float32 [4096], replicated, may hold values from 0.1 to 1.9
Outputs:
- normed: bfloat16 [2048, 4096], P(('seq', 'head'))
The draws below stay inside these ranges and needn't reach their ends.
Inputs may be any that keep to these rules, and one draw needn't show every extreme that they name: `values_in`: values of order one whose typical size differs from column to column.
All inputs are finite; a program needn't handle non-finite values.
Results may differ from the reference program's by a relative error of at most 0.0058.
Values may be sent and summed in bfloat16 or wider, within the bound.
No kernel may reach another device: no remote copies, remote signals or barrier semaphores. Data moves between devices by JAX's collectives and lax.ppermute only.
A program may use at most 128 MiB of HBM per device.

```python
import math
import jax
import jax.numpy as jnp
from jax import lax

H = 32
HD = 128
D = 4096
TOK_DEV = 64
TOKENS = 2048
N_SEQ = 8
N_HEAD = 4


def draw_values_in(key, part):
    first, second = jax.random.split(key, 2)
    column_scale = jnp.exp(jax.random.uniform(first, (D,), jnp.float32, math.log(0.3), math.log(3.0)))
    base = jax.random.normal(second, (TOKENS, D), jnp.float32)
    return jnp.clip(base * column_scale[None, :], -8.0, 8.0).astype(jnp.bfloat16)


def levels(key, shape, cuts, smallest, high):
    def one(dim, shards_of):
        heights = jax.random.uniform(jax.random.fold_in(jax.random.fold_in(key, 6), dim), (shards_of,), jnp.float32, smallest / len(cuts), high / len(cuts))
        return jnp.repeat(jnp.exp(heights), shape[dim] // shards_of).reshape((-1,) + (1,) * (len(shape) - dim - 1))

    level = one(*cuts[0])
    for cut in cuts[1:]:
        level = level * one(*cut)
    return level


def scatter_about(key, extent, scale, bound, shards=(), kind=jnp.bfloat16):
    level = levels(key, extent, shards, -0.22, 0.18) if shards else 1.0
    values = jax.random.normal(key, extent, jnp.float32) * scale * level
    return jnp.minimum(jnp.maximum(values, -bound), bound).astype(kind)


def setup_inputs(seed: int = 0) -> dict:
    key_of = jax.random.split(jax.random.key(seed), 5)
    return {
        "queries": scatter_about(key_of[0], (TOKENS, D), 1.0, 6.0, ((0, 32),)),
        "keys_in": scatter_about(key_of[1], (TOKENS, D), 1.0, 6.0, ((0, 32),)),
        "values_in": draw_values_in(jax.random.fold_in(key_of[4], 71), 0),
        "gain": jnp.clip(1.0 + 0.18 * jax.random.normal(key_of[3], (D,), jnp.float32), 0.1, 1.9),
    }


def reference(queries, keys_in, values_in, gain):
    shard_len = TOK_DEV * N_HEAD
    blocks = N_SEQ
    q_act = jax.nn.silu(queries.astype(jnp.float32)).astype(jnp.bfloat16).reshape(blocks, shard_len, H, HD)
    k_act = jax.nn.silu(keys_in.astype(jnp.float32)).astype(jnp.bfloat16).reshape(blocks, shard_len, H, HD)
    values = values_in.reshape(blocks, shard_len, H, HD)
    causal_mask = jnp.tril(jnp.ones((shard_len, shard_len), dtype=bool))

    def advance(carry_state, pieces):
        q_blk, k_blk, v_blk = pieces
        scores = jnp.einsum('thd,shd->hts', q_blk.astype(jnp.float32), k_blk.astype(jnp.float32))
        weights = jnp.where(causal_mask[None], scores, 0.0).astype(jnp.bfloat16)
        intra = jnp.einsum('hts,shd->thd', weights.astype(jnp.float32), v_blk.astype(jnp.float32))
        prefix = carry_state.astype(jnp.bfloat16)
        inter = jnp.einsum('thd,hde->the', q_blk.astype(jnp.float32), prefix.astype(jnp.float32))
        local_state = jnp.einsum('shd,she->hde', k_blk.astype(jnp.float32), v_blk.astype(jnp.float32))
        attn = (intra + inter).astype(jnp.bfloat16)
        return (carry_state + local_state, attn)
    start_state = jnp.zeros((H, HD, HD), jnp.float32)
    _, attn = lax.scan(advance, start_state, (q_act, k_act, values))
    widened = attn.reshape(TOKENS, D).astype(jnp.float32)
    mean_square = lax.optimization_barrier(jnp.mean(widened * widened, axis=-1, keepdims=True))
    return (widened * lax.rsqrt(mean_square + 1e-05) * gain[None, :]).astype(jnp.bfloat16)
```

```python
import functools

import jax
import jax.numpy as jnp
from jax import lax
from jax.experimental import pallas as pl
from jax.experimental.pallas import tpu as pltpu
from jax.sharding import PartitionSpec as P

HD = 128
AXES = ("seq", "head")


def divisor(count, most):
    found = 1
    while found < most and count % (2 * found) == 0:
        found *= 2
    return found


def silu(x):
    x = x.astype(jnp.float32)
    return (x / (1.0 + jnp.exp(-x))).astype(jnp.bfloat16)


def column(half, block, inner, blocks, per_block):
    head = (half * blocks + block) * per_block + inner
    return pl.ds(pl.multiple_of(head * HD, HD), HD)


def state_kernel(blocks, per_block, place_ref, k_ref, v_ref, keep_ref, send_ref):
    core, chip = place_ref[0], place_ref[1]
    for out_ref, half in ((send_ref, 1 - core), (keep_ref, core)):
        for d in range(blocks):
            for j in range(per_block):
                cols = column(half, chip ^ d, j, blocks, per_block)
                state = lax.dot_general(
                    silu(k_ref[:, cols]),
                    v_ref[:, cols],
                    (((0,), (0,)), ((), ())),
                    preferred_element_type=jnp.float32,
                )
                out_ref[d, j] = state.astype(out_ref.dtype)


def intra_kernel(q_ref, k_ref, v_ref, act_ref, intra_ref):
    rows = q_ref.shape[0]
    seen = lax.broadcasted_iota(jnp.int32, (rows, rows), 1) <= lax.broadcasted_iota(
        jnp.int32, (rows, rows), 0
    )
    for head in range(q_ref.shape[1] // HD):
        cols = pl.ds(head * HD, HD)
        q_act = silu(q_ref[:, cols])
        act_ref[:, cols] = q_act
        scores = lax.dot_general(
            q_act,
            silu(k_ref[:, cols]),
            (((1,), (1,)), ((), ())),
            preferred_element_type=jnp.float32,
        )
        weights = jnp.where(seen, scores, 0.0).astype(jnp.bfloat16)
        intra_ref[:, cols] = jnp.dot(
            weights, v_ref[:, cols], preferred_element_type=jnp.float32
        )


def finish_kernel(
    blocks, per_block, place_ref, act_ref, intra_ref, mine_ref, other_ref, gain_ref, out_ref, attn_ref
):
    core, chip = place_ref[0], place_ref[1]
    squares = jnp.zeros((act_ref.shape[0], HD), jnp.float32)
    for in_ref, half in ((mine_ref, core), (other_ref, 1 - core)):
        for d in range(blocks):
            for j in range(per_block):
                cols = column(half, chip ^ d, j, blocks, per_block)
                inter = jnp.dot(
                    act_ref[:, cols], in_ref[d, j], preferred_element_type=jnp.float32
                )
                attn = (intra_ref[:, cols] + inter).astype(jnp.bfloat16).astype(jnp.float32)
                attn_ref[:, cols] = attn
                squares += attn * attn
    mean = jnp.sum(squares, axis=1, keepdims=True) / act_ref.shape[1]
    scale = lax.rsqrt(mean + 1e-05)
    for head in range(act_ref.shape[1] // HD):
        cols = pl.ds(head * HD, HD)
        out_ref[:, cols] = (attn_ref[:, cols] * scale * gain_ref[:, cols]).astype(out_ref.dtype)


def local(count, queries, keys_in, values_in, gain):
    rows, features = queries.shape
    heads = features // HD
    pair = divisor(count, 2)
    blocks = divisor(count // pair, 4)
    upper = count // (pair * blocks)
    per_block = heads // (pair * blocks)
    assert pair == 2 and upper & (upper - 1) == 0
    f32, bf16 = jnp.float32, jnp.bfloat16

    me = lax.axis_index(AXES)
    core, chip = me % pair, (me // pair) % blocks
    place = jnp.stack([core, chip]).astype(jnp.int32)

    def swap(value, bit):
        return lax.ppermute(value, AXES, [(i, i ^ bit) for i in range(count)])

    vmem = pl.BlockSpec(memory_space=pltpu.VMEM)
    smem = pl.BlockSpec(memory_space=pltpu.SMEM)
    half = (blocks, per_block, HD, HD)
    flops = 2 * rows * features * HD
    size = rows * features * 2

    keep, send = pl.pallas_call(
        functools.partial(state_kernel, blocks, per_block),
        out_shape=(jax.ShapeDtypeStruct(half, f32), jax.ShapeDtypeStruct(half, f32)),
        in_specs=[smem, vmem, vmem],
        out_specs=(vmem, vmem),
        cost_estimate=pl.CostEstimate(
            flops=flops, bytes_accessed=4 * size, transcendentals=rows * features
        ),
        name="states",
    )(place, keys_in, values_in)
    received = swap(send, 1)

    act, intra = pl.pallas_call(
        intra_kernel,
        out_shape=(
            jax.ShapeDtypeStruct((rows, features), bf16),
            jax.ShapeDtypeStruct((rows, features), f32),
        ),
        in_specs=[vmem] * 3,
        out_specs=(vmem, vmem),
        cost_estimate=pl.CostEstimate(
            flops=2 * flops, bytes_accessed=6 * size, transcendentals=2 * rows * features
        ),
        name="intra",
    )(queries, keys_in, values_in)

    both = keep + received
    parts = [both[0]] + [
        swap(both[d].astype(bf16), pair * d).astype(f32) for d in range(1, blocks)
    ]

    total = functools.reduce(jnp.add, parts)
    before = jnp.zeros_like(total)
    bit = pair * blocks
    while bit < count:
        arrived = swap(total.astype(bf16), bit).astype(f32)
        before = before + jnp.where((me & bit) != 0, arrived, 0.0)
        total = total + arrived
        bit *= 2

    def entering(d):
        value = before
        for other in range(blocks):
            if other != d:
                value = value + jnp.where((chip ^ other) < (chip ^ d), parts[other], 0.0)
        return value.astype(bf16)

    back = [entering(0)] + [swap(entering(d), pair * d) for d in range(1, blocks)]
    prefix = jnp.stack(back).astype(f32)
    first = core == 0
    mine = (prefix + jnp.where(first, 0.0, received)).astype(bf16)
    other = swap((prefix + jnp.where(first, keep, 0.0)).astype(bf16), 1)

    return pl.pallas_call(
        functools.partial(finish_kernel, blocks, per_block),
        out_shape=jax.ShapeDtypeStruct((rows, features), bf16),
        in_specs=[smem] + [vmem] * 5,
        out_specs=vmem,
        scratch_shapes=[pltpu.VMEM((rows, features), f32)],
        cost_estimate=pl.CostEstimate(
            flops=flops, bytes_accessed=8 * size, transcendentals=rows
        ),
        name="finish",
    )(place, act, intra, mine, other, gain.reshape(1, features))


def solution(mesh):
    placed = P(AXES, None)
    count = mesh.shape["seq"] * mesh.shape["head"]
    return jax.shard_map(
        functools.partial(local, count),
        mesh=mesh,
        in_specs=(placed, placed, placed, P()),
        out_specs=placed,
        check_vma=False,
    )
```
